128 devices in a mesh: grp: 8 (over y, z_lo), dev: 16 (over x, z_hi, core).
Axes of the slice: x: 4, y: 4, z: 4 (z_hi: 2, z_lo: 2; z = z_hi * 2 + z_lo), core: 2. Of those that a mesh axis runs over, the one named last changes fastest.
Arguments:
- table: bfloat16 [8, 131072, 256], P('grp', 'dev'), may hold values from -0.75 to 0.75
- token_ids: int32 [32768], P(('grp', 'dev')), may hold values from 0 to 131071, as said below
- hidden: bfloat16 [32768, 2560], P(('grp', 'dev')), may hold values from -6 to 6
- w_proj: bfloat16 [2560, 2048], replicated, may hold values from -0.125 to 0.125
- norm_gain: float32 [256], replicated, may hold values from 0.5 to 1.5
Outputs:
- served_table: bfloat16 [16, 8, 1024, 2048], P('dev', 'grp')
- layer_inputs: bfloat16 [32768, 8, 256], P(('grp', 'dev'))
The draws below stay inside these ranges and needn't reach their ends.
Inputs may be any that keep to these rules, and one draw needn't show every extreme that they name: `token_ids`: of the 256 tokens of one device, at most 4 have ids in any one aligned block of 1024 vocabulary rows, and exactly 4 in some block.
All inputs are finite; a program needn't handle non-finite values.
Results may differ from the reference program's by a relative error of at most 0.001.
Values may be sent and summed in bfloat16 or wider, within the bound.
No kernel may reach another device: no remote copies, remote signals or barrier semaphores. Data moves between devices by JAX's collectives and lax.ppermute only.
A program may use at most 128 MiB of HBM per device.

```python
import math
import jax
import jax.numpy as jnp
from jax import lax

D = 2560
E = 256
LAYERS = 8
ROWS_DEV = 1024
TOK_DEV = 256
CAP = 4
VOCAB = 131072
TOKENS = 32768
N_GRP = 8
N_DEV = 16


def draw_token_ids(key, part):
    blocks = VOCAB // ROWS_DEV
    slots = blocks * CAP
    ranking = jax.random.permutation(jax.random.fold_in(key, 7), blocks).astype(jnp.int32)
    hotness = (ranking < max(blocks // 8, 1)).astype(jnp.int32)
    slot_ids = jnp.arange(slots, dtype=jnp.int32)
    slot_block = slot_ids // CAP

    def one_device(dev_key):
        key_full, key_score, key_order, key_first, key_second = jax.random.split(dev_key, 5)
        full_block = jax.random.randint(key_full, (), 0, blocks, dtype=jnp.int32)
        score = jax.random.randint(key_score, (slots,), 0, slots, dtype=jnp.int32) * slots + slot_ids
        score = score + jnp.take(hotness, slot_block) * slots * slots
        score = score + (slot_block == full_block).astype(jnp.int32) * 2 * slots * slots
        top_scores, chosen = lax.top_k(score, TOK_DEV)
        owners = (chosen.astype(jnp.int32) // CAP).astype(jnp.int32)
        order = jax.random.permutation(key_order, TOK_DEV)
        owners = owners[order]
        first = jax.random.randint(key_first, (TOK_DEV,), 0, ROWS_DEV, dtype=jnp.int32)
        second = jax.random.randint(key_second, (TOK_DEV,), 0, ROWS_DEV, dtype=jnp.int32)
        return owners * ROWS_DEV + jnp.minimum(first, second)
    dev_keys = jax.random.split(jax.random.fold_in(key, 11), blocks)
    return jax.vmap(one_device)(dev_keys).reshape(TOKENS).astype(jnp.int32)


def block_levels(stream_key, dims, pieces, low, top_value):
    loudness, own = 1.0, jax.random.fold_in(stream_key, 6)
    for position, parts in pieces:
        steps = jnp.exp(jax.random.uniform(jax.random.fold_in(own, position), (parts,), jnp.float32, low / len(pieces), top_value / len(pieces)))
        loudness = loudness * jnp.repeat(steps, dims[position] // parts).reshape([-1 if axis == position else 1 for axis in range(len(dims))])
    return loudness


def bell_draw(rng, extent, width, most, cuts=(), held_as=jnp.bfloat16):
    drawn = jax.random.normal(rng, extent, jnp.float32) * width
    if len(cuts) > 0:
        drawn = block_levels(rng, extent, cuts, -0.22, 0.18) * drawn
    return jnp.clip(drawn, min=-most, max=most).astype(held_as)


def setup_inputs(seed: int = 0) -> dict:
    seeds = jax.random.split(jax.random.key(seed), 6)
    table = bell_draw(seeds[0], (LAYERS, VOCAB, E), 0.125, 0.75, ((0, 8), (1, 16)))
    token_ids = draw_token_ids(jax.random.fold_in(seeds[5], 71), 0)
    hidden = bell_draw(seeds[2], (TOKENS, D), 1.0, 6.0, ((0, 128),))
    w_proj = bell_draw(seeds[3], (D, LAYERS * E), D ** -0.5, 0.125)
    norm_gain = jnp.clip(1.0 + 0.1 * jax.random.normal(seeds[4], (E,), jnp.float32), 0.5, 1.5)
    return dict(table=table, token_ids=token_ids, hidden=hidden, w_proj=w_proj, norm_gain=norm_gain)


def reference(table, token_ids, hidden, w_proj, norm_gain):
    served_table = jnp.transpose(table, (1, 0, 2)).reshape(N_DEV, N_GRP, ROWS_DEV, LAYERS * E)
    emb = jnp.transpose(jnp.take(table, token_ids, axis=1), (1, 0, 2)).astype(jnp.float32)
    proj = jnp.dot(hidden, w_proj, preferred_element_type=jnp.float32).reshape(TOKENS, LAYERS, E)
    mean_sq = lax.optimization_barrier(jnp.mean(proj * proj, axis=-1, keepdims=True))
    normed = proj / jnp.sqrt(mean_sq + 1e-06) * norm_gain
    layer_inputs = ((normed + math.sqrt(E) * emb) / math.sqrt(2.0)).astype(jnp.bfloat16)
    return (served_table, layer_inputs)
```

```python
import math

import jax
import jax.numpy as jnp
from jax import lax
from jax.experimental import pallas as pl
from jax.experimental.pallas import tpu as pltpu
from jax.sharding import PartitionSpec as P

CAP = 4


def rows_side_by_side(stacked):
    layers, rows, width = stacked.shape

    def body(x_ref, o_ref):
        o_ref[...] = x_ref[0]

    return pl.pallas_call(
        body,
        grid=(layers,),
        in_specs=[pl.BlockSpec((1, rows, width), lambda l: (l, 0, 0))],
        out_specs=pl.BlockSpec((rows, width), lambda l: (0, l)),
        out_shape=jax.ShapeDtypeStruct((rows, layers * width), stacked.dtype),
        cost_estimate=pl.CostEstimate(
            flops=0, bytes_accessed=2 * stacked.size * 2, transcendentals=0
        ),
    )(stacked)


def normed_projection(hidden, w_proj, norm_gain, layers):
    tok, depth = hidden.shape
    width = w_proj.shape[1] // layers

    def body(h_ref, w_ref, g_ref, o_ref):
        proj = jnp.dot(h_ref[...], w_ref[...], preferred_element_type=jnp.float32)
        mean_sq = jnp.mean(proj * proj, axis=-1, keepdims=True)
        o_ref[0] = proj / jnp.sqrt(mean_sq + 1e-06) * g_ref[...]

    return pl.pallas_call(
        body,
        grid=(layers,),
        in_specs=[
            pl.BlockSpec((tok, depth), lambda l: (0, 0)),
            pl.BlockSpec((depth, width), lambda l: (0, l)),
            pl.BlockSpec((1, width), lambda l: (0, 0)),
        ],
        out_specs=pl.BlockSpec((1, tok, width), lambda l: (l, 0, 0)),
        out_shape=jax.ShapeDtypeStruct((layers, tok, width), jnp.float32),
        cost_estimate=pl.CostEstimate(
            flops=2 * tok * depth * layers * width,
            bytes_accessed=2 * depth * (tok + layers * width) + 4 * tok * layers * width,
            transcendentals=0,
        ),
    )(hidden, w_proj, norm_gain.reshape(1, width))


def pick_and_add(slots, replies, normed):
    layers, count, width = replies.shape
    tok = normed.shape[1]

    def body(s_ref, r_ref, n_ref, o_ref, acc_ref):
        picker = (
            s_ref[...] == lax.broadcasted_iota(jnp.int32, (tok, count), 1)
        ).astype(jnp.bfloat16)
        for l in range(layers):
            emb = jnp.dot(picker, r_ref[l], preferred_element_type=jnp.float32)
            acc_ref[:, l, :] = (n_ref[l] + math.sqrt(width) * emb) / math.sqrt(2.0)
        o_ref[...] = acc_ref[...].astype(jnp.bfloat16)

    return pl.pallas_call(
        body,
        out_shape=jax.ShapeDtypeStruct((tok, layers, width), jnp.bfloat16),
        scratch_shapes=[pltpu.VMEM((tok, layers, width), jnp.float32)],
        cost_estimate=pl.CostEstimate(
            flops=2 * tok * count * layers * width,
            bytes_accessed=2 * layers * width * (count + 3 * tok),
            transcendentals=0,
        ),
    )(slots.reshape(tok, 1), replies, normed)


def on_device(table, token_ids, hidden, w_proj, norm_gain):
    n_grp = lax.axis_size("grp")
    n_dev = lax.axis_size("dev")
    peers = n_grp * n_dev
    _, shard_rows, width = table.shape
    layers = w_proj.shape[1] // width
    row_count = shard_rows // n_grp
    tok_count = token_ids.shape[0]
    blocks = peers
    slots = blocks * CAP
    dev_slots = slots // n_dev
    both = ("grp", "dev")

    owner = token_ids // row_count
    positions = jnp.arange(tok_count, dtype=jnp.int32)
    same = (owner[:, None] == owner[None, :]) & (positions[None, :] < positions[:, None])
    slot = owner * CAP + jnp.sum(same.astype(jnp.int32), axis=1)
    hit = (slot[:, None] == jnp.arange(slots, dtype=jnp.int32)[None, :]).astype(jnp.int32)
    local = token_ids % row_count
    outgoing = (jnp.sum(hit * (local + 1)[:, None], axis=0) - 1).reshape(1, n_dev, dev_slots)
    outgoing = jnp.broadcast_to(outgoing, (n_grp, n_dev, dev_slots)).reshape(peers, dev_slots)
    incoming = lax.all_to_all(outgoing, both, split_axis=0, concat_axis=0, tiled=True)

    shard = table.reshape(n_grp, row_count, width)
    gated, incoming = lax.optimization_barrier((shard, incoming))
    moved = lax.all_to_all(gated, "grp", split_axis=0, concat_axis=0, tiled=True)

    wanted = incoming.reshape(peers, n_grp, CAP).transpose(1, 0, 2).reshape(n_grp, peers * CAP)
    onehot = (
        wanted[:, :, None] == jnp.arange(row_count, dtype=jnp.int32)[None, None, :]
    ).astype(jnp.bfloat16)
    found = lax.dot_general(
        onehot, shard, (((2,), (1,)), ((0,), (0,))), preferred_element_type=jnp.float32
    ).astype(jnp.bfloat16)
    found = found.reshape(n_grp, peers, CAP, width).transpose(1, 0, 2, 3)
    found = found.reshape(peers, dev_slots, width)
    normed = normed_projection(hidden, w_proj, norm_gain, layers)
    moved, found, normed = lax.optimization_barrier((moved, found, normed))

    replies = lax.all_to_all(found, both, split_axis=0, concat_axis=0, tiled=True)
    served = rows_side_by_side(moved).reshape(1, 1, row_count, layers * width)
    layer_inputs = pick_and_add(slot, replies.reshape(layers, slots, width), normed)
    return (served, layer_inputs)


def solution(mesh):
    in_specs = (P("grp", "dev", None), P(("grp", "dev")), P(("grp", "dev"), None), P(), P())
    out_specs = (P("dev", "grp", None, None), P(("grp", "dev"), None, None))
    return jax.shard_map(
        on_device, mesh=mesh, in_specs=in_specs, out_specs=out_specs, check_vma=False
    )
```

```python
import functools
import math

import jax
import jax.numpy as jnp
from jax import lax
from jax.experimental import pallas as pl
from jax.experimental.pallas import tpu as pltpu
from jax.sharding import PartitionSpec as P

CAP = 4
LANES = 128
BOTH = ("grp", "dev")


def flat_index(y, zl, x, zh, c, n_x):
    return (y * 2 + zl) * (n_x * 4) + x * 4 + zh * 2 + c


def send(value, n_y, n_x, dx=0, flip=0, core=0):
    moves = []
    for y in range(n_y):
        for x in range(n_x):
            for rest in range(8):
                zl, zh, c = rest // 4, rest // 2 % 2, rest % 2
                here = flat_index(y, zl, x, zh, c, n_x)
                there = flat_index(y, zl ^ flip, (x + dx) % n_x, zh ^ flip, c ^ core, n_x)
                moves.append((here, there))
    return lax.ppermute(value, BOTH, moves)


def rows_side_by_side(stacked):
    layers, rows, width = stacked.shape

    def body(x_ref, o_ref):
        o_ref[...] = x_ref[0]

    return pl.pallas_call(
        body,
        grid=(layers,),
        in_specs=[pl.BlockSpec((1, rows, width), lambda l: (l, 0, 0))],
        out_specs=pl.BlockSpec((rows, width), lambda l: (0, l)),
        out_shape=jax.ShapeDtypeStruct((rows, layers * width), stacked.dtype),
        cost_estimate=pl.CostEstimate(
            flops=0, bytes_accessed=2 * stacked.size * 2, transcendentals=0
        ),
    )(stacked)


def column_of(line):
    lanes = line.shape[1]
    return jnp.transpose(jnp.broadcast_to(line, (lanes, lanes)))


def onehot_of(line, depth):
    col = column_of(line)
    lane = lax.broadcasted_iota(jnp.int32, col.shape, 1)
    return jnp.concatenate(
        [(col == lane + k * LANES).astype(jnp.bfloat16) for k in range(depth // LANES)], axis=1
    )


def look_up(shard, wanted, n_x, n_grp, first, x_first):
    pairs, lines, lanes = wanted.shape
    rows, width = shard.shape
    depth = rows // pairs
    half = pairs // 2
    run = 2 * CAP
    outs = (n_x, 2) if x_first else (2, n_x)

    def body(w_ref, t_ref, *o_refs):
        for r in range(lines):
            kx, s = r // 2, r % 2
            got = jnp.dot(
                onehot_of(w_ref[0, r : r + 1, :], depth),
                t_ref[...],
                preferred_element_type=jnp.float32,
            )
            got = got.reshape(2, n_grp, run, width).astype(jnp.bfloat16)
            if x_first:
                o_refs[kx][s] = got
            else:
                o_refs[s][kx] = got

    return pl.pallas_call(
        body,
        grid=(half,),
        in_specs=[
            pl.BlockSpec((1, lines, lanes), lambda p: (p + first, 0, 0)),
            pl.BlockSpec((depth, width), lambda p: (p + first, 0)),
        ],
        out_specs=[
            pl.BlockSpec((outs[1], 2, n_grp, run, width), lambda p: (0, 0, 0, p, 0))
        ]
        * outs[0],
        out_shape=[
            jax.ShapeDtypeStruct((outs[1], 2, n_grp, half * run, width), jnp.bfloat16)
        ]
        * outs[0],
        cost_estimate=pl.CostEstimate(
            flops=2 * half * lines * lanes * depth * width,
            bytes_accessed=2 * half * (depth + lines * lanes) * width,
            transcendentals=0,
        ),
    )(wanted, shard)


def in_token_order(own, other, places):
    n_grp, tok = places.shape
    width = own.shape[-1]
    run = own.shape[-2]
    parts = own.size // (n_grp * run * width)
    count = 2 * parts * run

    def body(p_ref, a_ref, b_ref, o_ref):
        rows = jnp.concatenate(
            [a_ref[i, 0] for i in range(parts)] + [b_ref[i, 0] for i in range(parts)], axis=0
        )
        for t in range(tok // LANES):
            line = p_ref[0, :, t * LANES : (t + 1) * LANES]
            got = jnp.dot(onehot_of(line, count), rows, preferred_element_type=jnp.float32)
            o_ref[0, t * LANES : (t + 1) * LANES] = got.astype(jnp.bfloat16)

    piece = pl.BlockSpec((parts, 1, run, width), lambda g: (0, g, 0, 0))
    return pl.pallas_call(
        body,
        grid=(n_grp,),
        in_specs=[pl.BlockSpec((1, 1, tok), lambda g: (g, 0, 0)), piece, piece],
        out_specs=pl.BlockSpec((1, tok, width), lambda g: (g, 0, 0)),
        out_shape=jax.ShapeDtypeStruct((n_grp, tok, width), jnp.bfloat16),
        cost_estimate=pl.CostEstimate(
            flops=2 * n_grp * tok * count * width,
            bytes_accessed=2 * n_grp * (count + tok) * width,
            transcendentals=0,
        ),
    )(
        places.reshape(n_grp, 1, tok),
        own.reshape(parts, n_grp, run, width),
        other.reshape(parts, n_grp, run, width),
    )


def normed_projection(hidden, w_proj, norm_gain, layers):
    tok, depth = hidden.shape
    width = w_proj.shape[1] // layers

    def body(h_ref, w_ref, g_ref, o_ref):
        proj = jnp.dot(h_ref[...], w_ref[...], preferred_element_type=jnp.float32)
        mean_sq = jnp.mean(proj * proj, axis=-1, keepdims=True)
        o_ref[0] = proj / jnp.sqrt(mean_sq + 1e-06) * g_ref[...]

    return pl.pallas_call(
        body,
        grid=(layers,),
        in_specs=[
            pl.BlockSpec((tok, depth), lambda l: (0, 0)),
            pl.BlockSpec((depth, width), lambda l: (0, l)),
            pl.BlockSpec((1, width), lambda l: (0, 0)),
        ],
        out_specs=pl.BlockSpec((1, tok, width), lambda l: (l, 0, 0)),
        out_shape=jax.ShapeDtypeStruct((layers, tok, width), jnp.float32),
        cost_estimate=pl.CostEstimate(
            flops=2 * tok * depth * layers * width,
            bytes_accessed=2 * depth * (tok + layers * width) + 4 * tok * layers * width,
            transcendentals=0,
        ),
    )(hidden, w_proj, norm_gain.reshape(1, width))


def add_embedding(crossed, pieces, normed):
    layers, tok, width = pieces.shape

    def body(s_ref, r_ref, n_ref, o_ref, acc_ref):
        swap = s_ref[...] > 0
        for l in range(layers):
            emb = jnp.where(
                swap, r_ref[l ^ 1].astype(jnp.float32), r_ref[l].astype(jnp.float32)
            )
            acc_ref[:, l, :] = (n_ref[l] + math.sqrt(width) * emb) / math.sqrt(2.0)
        o_ref[...] = acc_ref[...].astype(jnp.bfloat16)

    vmem = pl.BlockSpec(memory_space=pltpu.VMEM)
    return pl.pallas_call(
        body,
        in_specs=[vmem, vmem, vmem],
        out_specs=vmem,
        out_shape=jax.ShapeDtypeStruct((tok, layers, width), jnp.bfloat16),
        scratch_shapes=[pltpu.VMEM((tok, layers, width), jnp.float32)],
        compiler_params=pltpu.CompilerParams(vmem_limit_bytes=16 << 20),
        cost_estimate=pl.CostEstimate(
            flops=6 * tok * layers * width,
            bytes_accessed=8 * layers * width * tok,
            transcendentals=0,
        ),
    )(crossed.reshape(tok, 1), pieces, normed)


def on_device(table, token_ids, hidden, w_proj, norm_gain):
    n_grp = lax.axis_size("grp")
    n_dev = lax.axis_size("dev")
    n_y, n_x = n_grp // 2, n_dev // 4
    peers = n_grp * n_dev
    d_index = lax.axis_index("dev")
    my_x, my_zh, my_c = d_index // 4, d_index // 2 % 2, d_index % 2
    _, shard_rows, width = table.shape
    layers = w_proj.shape[1] // width
    row_count = shard_rows // n_grp
    tok_count = token_ids.shape[0]
    slots = peers * CAP
    dev_slots = slots // n_dev
    pairs = n_grp // 2
    shard = table.reshape(shard_rows, width)
    hop = functools.partial(send, n_y=n_y, n_x=n_x)

    block = token_ids // row_count
    positions = jnp.arange(tok_count, dtype=jnp.int32)
    same = (block[:, None] == block[None, :]) & (positions[None, :] < positions[:, None])
    rank = jnp.sum(same.astype(jnp.int32), axis=1)
    slot = block * CAP + rank
    hit = (slot[:, None] == jnp.arange(slots, dtype=jnp.int32)[None, :]).astype(jnp.int32)
    local = token_ids % (2 * row_count)
    requests = (jnp.sum(hit * (local + 1)[:, None], axis=0) - 1).reshape(1, n_dev, dev_slots)
    holder = block // n_grp
    k = (my_x - holder // 4 + n_x) % n_x
    crossed = (holder // 2 % 2) ^ my_zh
    kc = (holder % 2) ^ my_c
    in_shard = block % n_grp
    half_run = n_grp // 2 * CAP
    place = kc * 2 + in_shard // (n_grp // 2)
    place = (place * 2 + crossed) * n_x + k
    place = place * half_run + in_shard % (n_grp // 2) * CAP + rank
    outgoing = jnp.concatenate(
        [
            jnp.broadcast_to(requests, (n_grp, n_dev, dev_slots)).reshape(peers, dev_slots),
            jnp.broadcast_to(place[None], (peers, tok_count)),
        ],
        axis=1,
    )
    incoming = lax.all_to_all(outgoing, BOTH, split_axis=0, concat_axis=0, tiled=True)

    gated, incoming = lax.optimization_barrier((table.reshape(n_grp, row_count, width), incoming))
    moved = lax.all_to_all(gated, "grp", split_axis=0, concat_axis=0, tiled=True)

    places = lax.dynamic_index_in_dim(
        incoming.reshape(n_grp, n_dev, dev_slots + tok_count)[:, :, dev_slots:], d_index, 1, False
    )
    asked = incoming[:, :dev_slots].reshape(n_grp, n_x, 2, 2, pairs, 2 * CAP)
    asked = lax.dynamic_slice_in_dim(jnp.concatenate([asked, asked], axis=1), my_x, n_x, 1)
    asked = jnp.where(my_zh == 1, asked[:, :, ::-1], asked)
    asked = jnp.where(my_c == 1, asked[:, :, :, ::-1], asked)
    wanted = asked.transpose(4, 1, 2, 3, 0, 5).reshape(pairs, n_x * 2, 2 * n_grp * 2 * CAP)

    to_x = look_up(shard, wanted, n_x, n_grp, 0, True)
    near, far = look_up(shard, wanted, n_x, n_grp, pairs // 2, False)
    a_x = [to_x[0]] + [hop(to_x[q], dx=q) for q in range(1, n_x)]
    b_far = hop(far, flip=1)
    a_far = hop(jnp.stack([a[1] for a in a_x]), flip=1)
    b_x = [jnp.stack([near[0], b_far[0]])]
    for q in range(1, n_x):
        b_x.append(hop(jnp.stack([near[q], b_far[q]]), dx=q))
    held = jnp.stack(
        [
            jnp.stack([jnp.stack([a[0] for a in a_x]), a_far]),
            jnp.stack(b_x, axis=1),
        ]
    )
    own, other = held[:, :, :, 0], hop(held[:, :, :, 1], core=1)
    sorted_rows = in_token_order(own, other, places)
    normed = normed_projection(hidden, w_proj, norm_gain, layers)
    moved, sorted_rows, normed = lax.optimization_barrier((moved, sorted_rows, normed))

    pieces = lax.all_to_all(sorted_rows, "grp", split_axis=0, concat_axis=0, tiled=True)
    served = rows_side_by_side(moved).reshape(1, 1, row_count, layers * width)
    layer_inputs = add_embedding(crossed, pieces, normed)
    return (served, layer_inputs)


def solution(mesh):
    in_specs = (P("grp", "dev", None), P(("grp", "dev")), P(("grp", "dev"), None), P(), P())
    out_specs = (P("dev", "grp", None, None), P(("grp", "dev"), None, None))
    return jax.shard_map(
        on_device, mesh=mesh, in_specs=in_specs, out_specs=out_specs, check_vma=False
    )
```

```python
import functools
import math

import jax
import jax.numpy as jnp
from jax import lax
from jax.experimental import pallas as pl
from jax.experimental.pallas import tpu as pltpu
from jax.sharding import PartitionSpec as P

CAP = 4
LANES = 128
BOTH = ("grp", "dev")


def flat_index(y, zl, x, zh, c, n_x):
    return (y * 2 + zl) * (n_x * 4) + x * 4 + zh * 2 + c


def send(value, n_y, n_x, dx=0, flip=0, core=0):
    moves = []
    for y in range(n_y):
        for x in range(n_x):
            for rest in range(8):
                zl, zh, c = rest // 4, rest // 2 % 2, rest % 2
                here = flat_index(y, zl, x, zh, c, n_x)
                there = flat_index(y, zl ^ flip, (x + dx) % n_x, zh ^ flip, c ^ core, n_x)
                moves.append((here, there))
    return lax.ppermute(value, BOTH, moves)


def rows_side_by_side(stacked):
    layers, rows, width = stacked.shape

    def body(x_ref, o_ref):
        o_ref[...] = x_ref[0]

    return pl.pallas_call(
        body,
        grid=(layers,),
        in_specs=[pl.BlockSpec((1, rows, width), lambda l: (l, 0, 0))],
        out_specs=pl.BlockSpec((rows, width), lambda l: (0, l)),
        out_shape=jax.ShapeDtypeStruct((rows, layers * width), stacked.dtype),
        cost_estimate=pl.CostEstimate(
            flops=0, bytes_accessed=2 * stacked.size * 2, transcendentals=0
        ),
    )(stacked)


def column_of(line):
    lanes = line.shape[1]
    return jnp.transpose(jnp.broadcast_to(line, (lanes, lanes)))


def onehot_of(line, depth):
    col = column_of(line)
    lane = lax.broadcasted_iota(jnp.int32, col.shape, 1)
    return jnp.concatenate(
        [(col == lane + k * LANES).astype(jnp.bfloat16) for k in range(depth // LANES)], axis=1
    )


def look_up(shard, wanted, n_x, n_grp, first, x_first):
    pairs, lines, lanes = wanted.shape
    rows, width = shard.shape
    depth = rows // pairs
    half = pairs // 2
    run = 2 * CAP
    outs = (n_x, 2) if x_first else (2, n_x)

    def body(w_ref, t_ref, *o_refs):
        for r in range(lines):
            kx, s = r // 2, r % 2
            got = jnp.dot(
                onehot_of(w_ref[0, r : r + 1, :], depth),
                t_ref[...],
                preferred_element_type=jnp.float32,
            )
            got = got.reshape(2, n_grp, run, width).astype(jnp.bfloat16)
            if x_first:
                o_refs[kx][s] = got
            else:
                o_refs[s][kx] = got

    return pl.pallas_call(
        body,
        grid=(half,),
        in_specs=[
            pl.BlockSpec((1, lines, lanes), lambda p: (p + first, 0, 0)),
            pl.BlockSpec((depth, width), lambda p: (p + first, 0)),
        ],
        out_specs=[
            pl.BlockSpec((outs[1], 2, n_grp, run, width), lambda p: (0, 0, 0, p, 0))
        ]
        * outs[0],
        out_shape=[
            jax.ShapeDtypeStruct((outs[1], 2, n_grp, half * run, width), jnp.bfloat16)
        ]
        * outs[0],
        cost_estimate=pl.CostEstimate(flops=0, bytes_accessed=1 << 16, transcendentals=0),
    )(wanted, shard)


def near_call(body, outs, operands):
    vmem = pl.BlockSpec(memory_space=pltpu.VMEM)
    return pl.pallas_call(
        body,
        in_specs=[vmem] * len(operands),
        out_specs=[vmem] * len(outs),
        out_shape=[jax.ShapeDtypeStruct(shape, jnp.bfloat16) for shape in outs],
        compiler_params=pltpu.CompilerParams(vmem_limit_bytes=16 << 20),
        cost_estimate=pl.CostEstimate(flops=0, bytes_accessed=1 << 16, transcendentals=0),
    )(*operands)


def flip_parts(a_x):
    def body(*refs):
        for k, ref in enumerate(refs[:-1]):
            refs[-1][k] = ref[1]

    return near_call(body, [(len(a_x), *a_x[0].shape[1:])], a_x)[0]


def x_parts(near, b_far):
    n_x = near.shape[0]

    def body(n_ref, f_ref, *o_refs):
        for k, o_ref in enumerate(o_refs):
            o_ref[0] = n_ref[k + 1]
            o_ref[1] = f_ref[k + 1]

    return near_call(body, [(2, *near.shape[1:])] * (n_x - 1), [near, b_far])


def rows_by_core(refs, n_x, core, pick):
    a_refs, far_ref, near_ref, b_far_ref = refs[:n_x], refs[n_x], refs[n_x + 1], refs[n_x + 2]
    b_refs = refs[n_x + 3 : 2 * n_x + 2]
    rows = [r[(0, core) + pick] for r in a_refs]
    rows += [far_ref[(k, core) + pick] for k in range(n_x)]
    for s, ref in ((0, near_ref), (1, b_far_ref)):
        rows += [ref[(0, core) + pick]] + [r[(s, core) + pick] for r in b_refs]
    return rows


def core_parts(parts, n_x):
    def body(*refs):
        for i, rows in enumerate(rows_by_core(refs[:-1], n_x, 1, ())):
            refs[-1][i] = rows

    return near_call(body, [(4 * n_x, *parts[0].shape[2:])], parts)[0]


def in_token_order(places, parts, other, n_x):
    n_grp, tok = places.shape
    pieces, _, run, width = other.shape
    count = 2 * pieces * run

    def body(p_ref, *refs):
        o_ref, other_ref = refs[-1], refs[-2]
        for g in range(n_grp):
            rows = rows_by_core(refs[:-2], n_x, 0, (g,))
            rows += [other_ref[i, g] for i in range(pieces)]
            rows = jnp.concatenate(rows, axis=0)
            for t in range(tok // LANES):
                line = p_ref[g : g + 1, t * LANES : (t + 1) * LANES]
                got = jnp.dot(onehot_of(line, count), rows, preferred_element_type=jnp.float32)
                o_ref[g, t * LANES : (t + 1) * LANES] = got.astype(jnp.bfloat16)

    return near_call(body, [(n_grp, tok, width)], [places, *parts, other])[0]


def normed_projection(hidden, w_proj, norm_gain, layers):
    tok, depth = hidden.shape
    width = w_proj.shape[1] // layers

    def body(h_ref, w_ref, g_ref, o_ref):
        proj = jnp.dot(h_ref[...], w_ref[...], preferred_element_type=jnp.float32)
        mean_sq = jnp.mean(proj * proj, axis=-1, keepdims=True)
        o_ref[0] = proj / jnp.sqrt(mean_sq + 1e-06) * g_ref[...]

    return pl.pallas_call(
        body,
        grid=(layers,),
        in_specs=[
            pl.BlockSpec((tok, depth), lambda l: (0, 0)),
            pl.BlockSpec((depth, width), lambda l: (0, l)),
            pl.BlockSpec((1, width), lambda l: (0, 0)),
        ],
        out_specs=pl.BlockSpec((1, tok, width), lambda l: (l, 0, 0)),
        out_shape=jax.ShapeDtypeStruct((layers, tok, width), jnp.float32),
        cost_estimate=pl.CostEstimate(
            flops=2 * tok * depth * layers * width,
            bytes_accessed=2 * depth * (tok + layers * width) + 4 * tok * layers * width,
            transcendentals=0,
        ),
    )(hidden, w_proj, norm_gain.reshape(1, width))


def add_embedding(crossed, pieces, normed):
    layers, tok, width = pieces.shape

    def body(s_ref, r_ref, n_ref, o_ref, acc_ref):
        swap = s_ref[...] > 0
        for l in range(layers):
            emb = jnp.where(
                swap, r_ref[l ^ 1].astype(jnp.float32), r_ref[l].astype(jnp.float32)
            )
            acc_ref[:, l, :] = (n_ref[l] + math.sqrt(width) * emb) / math.sqrt(2.0)
        o_ref[...] = acc_ref[...].astype(jnp.bfloat16)

    vmem = pl.BlockSpec(memory_space=pltpu.VMEM)
    return pl.pallas_call(
        body,
        in_specs=[vmem, vmem, vmem],
        out_specs=vmem,
        out_shape=jax.ShapeDtypeStruct((tok, layers, width), jnp.bfloat16),
        scratch_shapes=[pltpu.VMEM((tok, layers, width), jnp.float32)],
        compiler_params=pltpu.CompilerParams(vmem_limit_bytes=16 << 20),
        cost_estimate=pl.CostEstimate(
            flops=6 * tok * layers * width,
            bytes_accessed=8 * layers * width * tok,
            transcendentals=0,
        ),
    )(crossed.reshape(tok, 1), pieces, normed)


def on_device(table, token_ids, hidden, w_proj, norm_gain):
    n_grp = lax.axis_size("grp")
    n_dev = lax.axis_size("dev")
    n_y, n_x = n_grp // 2, n_dev // 4
    peers = n_grp * n_dev
    d_index = lax.axis_index("dev")
    my_x, my_zh, my_c = d_index // 4, d_index // 2 % 2, d_index % 2
    _, shard_rows, width = table.shape
    layers = w_proj.shape[1] // width
    row_count = shard_rows // n_grp
    tok_count = token_ids.shape[0]
    slots = peers * CAP
    dev_slots = slots // n_dev
    pairs = n_grp // 2
    shard = table.reshape(shard_rows, width)
    hop = functools.partial(send, n_y=n_y, n_x=n_x)

    block = token_ids // row_count
    positions = jnp.arange(tok_count, dtype=jnp.int32)
    same = (block[:, None] == block[None, :]) & (positions[None, :] < positions[:, None])
    rank = jnp.sum(same.astype(jnp.int32), axis=1)
    slot = block * CAP + rank
    hit = (slot[:, None] == jnp.arange(slots, dtype=jnp.int32)[None, :]).astype(jnp.int32)
    local = token_ids % (2 * row_count)
    requests = (jnp.sum(hit * (local + 1)[:, None], axis=0) - 1).reshape(1, n_dev, dev_slots)
    holder = block // n_grp
    k = (my_x - holder // 4 + n_x) % n_x
    crossed = (holder // 2 % 2) ^ my_zh
    kc = (holder % 2) ^ my_c
    in_shard = block % n_grp
    half_run = n_grp // 2 * CAP
    place = kc * 2 + in_shard // (n_grp // 2)
    place = (place * 2 + crossed) * n_x + k
    place = place * half_run + in_shard % (n_grp // 2) * CAP + rank
    outgoing = jnp.concatenate(
        [
            jnp.broadcast_to(requests, (n_grp, n_dev, dev_slots)).reshape(peers, dev_slots),
            jnp.broadcast_to(place[None], (peers, tok_count)),
        ],
        axis=1,
    )
    incoming = lax.all_to_all(outgoing, BOTH, split_axis=0, concat_axis=0, tiled=True)

    normed = normed_projection(hidden, w_proj, norm_gain, layers)
    gated, incoming, normed = lax.optimization_barrier(
        (table.reshape(n_grp, row_count, width), incoming, normed)
    )
    moved = lax.all_to_all(gated, "grp", split_axis=0, concat_axis=0, tiled=True)

    places = lax.dynamic_index_in_dim(
        incoming.reshape(n_grp, n_dev, dev_slots + tok_count)[:, :, dev_slots:], d_index, 1, False
    )
    asked = incoming[:, :dev_slots].reshape(n_grp, n_x, 2, 2, pairs, 2 * CAP)
    asked = lax.dynamic_slice_in_dim(jnp.concatenate([asked, asked], axis=1), my_x, n_x, 1)
    asked = jnp.where(my_zh == 1, asked[:, :, ::-1], asked)
    asked = jnp.where(my_c == 1, asked[:, :, :, ::-1], asked)
    wanted = asked.transpose(4, 1, 2, 3, 0, 5).reshape(pairs, n_x * 2, 2 * n_grp * 2 * CAP)

    a_x = look_up(shard, wanted, n_x, n_grp, 0, True)
    near, far = look_up(shard, wanted, n_x, n_grp, pairs // 2, False)
    a_x = [a_x[0]] + [hop(a_x[q], dx=q) for q in range(1, n_x)]
    b_far = hop(far, flip=1)
    a_far = hop(flip_parts(a_x), flip=1)
    b_x = [hop(part, dx=q + 1) for q, part in enumerate(x_parts(near, b_far))]
    parts = [*a_x, a_far, near, b_far, *b_x]
    other = hop(core_parts(parts, n_x), core=1)
    sorted_rows = in_token_order(places, parts, other, n_x)
    moved, sorted_rows = lax.optimization_barrier((moved, sorted_rows))

    pieces = lax.all_to_all(sorted_rows, "grp", split_axis=0, concat_axis=0, tiled=True)
    served = rows_side_by_side(moved).reshape(1, 1, row_count, layers * width)
    layer_inputs = add_embedding(crossed, pieces, normed)
    return (served, layer_inputs)


def solution(mesh):
    in_specs = (P("grp", "dev", None), P(("grp", "dev")), P(("grp", "dev"), None), P(), P())
    out_specs = (P("dev", "grp", None, None), P(("grp", "dev"), None, None))
    return jax.shard_map(
        on_device, mesh=mesh, in_specs=in_specs, out_specs=out_specs, check_vma=False
    )
```

```python
import functools
import math

import jax
import jax.numpy as jnp
from jax import lax
from jax.experimental import pallas as pl
from jax.experimental.pallas import tpu as pltpu
from jax.sharding import PartitionSpec as P

CAP = 4
LANES = 128
BOTH = ("grp", "dev")


def flat_index(y, zl, x, zh, c, n_x):
    return (y * 2 + zl) * (n_x * 4) + x * 4 + zh * 2 + c


def send(value, n_y, n_x, dx=0, flip=0, core=0):
    moves = []
    for y in range(n_y):
        for x in range(n_x):
            for rest in range(8):
                zl, zh, c = rest // 4, rest // 2 % 2, rest % 2
                here = flat_index(y, zl, x, zh, c, n_x)
                there = flat_index(y, zl ^ flip, (x + dx) % n_x, zh ^ flip, c ^ core, n_x)
                moves.append((here, there))
    return lax.ppermute(value, BOTH, moves)


def column_of(line):
    lanes = line.shape[1]
    return jnp.transpose(jnp.broadcast_to(line, (lanes, lanes)))


def onehot_of(line, depth):
    col = column_of(line)
    lane = lax.broadcasted_iota(jnp.int32, col.shape, 1)
    return jnp.concatenate(
        [(col == lane + k * LANES).astype(jnp.bfloat16) for k in range(depth // LANES)], axis=1
    )


def look_up(shard, wanted, n_x, n_grp, x_first):
    blocks, lines, lanes = wanted.shape
    rows, width = shard.shape
    depth = rows // blocks
    half = blocks // 2
    duo = n_grp // 2
    outs = (n_x, 2) if x_first else (2, n_x)
    from_line, from_row = (0, half) if x_first else (half, 0)

    def body(w_ref, t_ref, *o_refs):
        for b in range(half):
            onehot = jnp.concatenate(
                [onehot_of(w_ref[from_line + b, r : r + 1, :], depth) for r in range(lines)],
                axis=0,
            )
            first = (from_row + b) * depth
            got = jnp.dot(
                onehot, t_ref[first : first + depth], preferred_element_type=jnp.float32
            )
            got = got.reshape(n_x, 2, 2, duo, 2 * CAP, width).astype(jnp.bfloat16)
            for k in range(n_x):
                for s in range(2):
                    if x_first:
                        o_refs[k][s, :, :, b] = got[k, s]
                    else:
                        o_refs[s][k, :, :, b] = got[k, s]

    shape = (outs[1], 2, duo, half, 2 * CAP, width)
    return near_call(body, [shape] * outs[0], [wanted, shard])


def near_call(body, outs, operands):
    vmem = pl.BlockSpec(memory_space=pltpu.VMEM)
    return pl.pallas_call(
        body,
        in_specs=[vmem] * len(operands),
        out_specs=[vmem] * len(outs),
        out_shape=[jax.ShapeDtypeStruct(shape, jnp.bfloat16) for shape in outs],
        compiler_params=pltpu.CompilerParams(vmem_limit_bytes=16 << 20),
        cost_estimate=pl.CostEstimate(flops=0, bytes_accessed=1 << 16, transcendentals=0),
    )(*operands)


def flip_parts(a_x):
    def body(*refs):
        for k, ref in enumerate(refs[:-1]):
            refs[-1][k] = ref[1]

    return near_call(body, [(len(a_x), *a_x[0].shape[1:])], a_x)[0]


def x_parts(near, b_far):
    n_x = near.shape[0]

    def body(n_ref, f_ref, *o_refs):
        for k, o_ref in enumerate(o_refs):
            o_ref[0] = n_ref[k + 1]
            o_ref[1] = f_ref[k + 1]

    return near_call(body, [(2, *near.shape[1:])] * (n_x - 1), [near, b_far])


def rows_by_core(refs, n_x, core, pick):
    a_refs, far_ref, near_ref, b_far_ref = refs[:n_x], refs[n_x], refs[n_x + 1], refs[n_x + 2]
    b_refs = refs[n_x + 3 : 2 * n_x + 2]
    rows = [r[(0, core) + pick] for r in a_refs]
    rows += [far_ref[(k, core) + pick] for k in range(n_x)]
    for s, ref in ((0, near_ref), (1, b_far_ref)):
        rows += [ref[(0, core) + pick]] + [r[(s, core) + pick] for r in b_refs]
    return rows


def core_parts(parts, n_x):
    def body(*refs):
        for i, rows in enumerate(rows_by_core(refs[:-1], n_x, 1, ())):
            refs[-1][i] = rows

    return near_call(body, [(4 * n_x, *parts[0].shape[2:])], parts)[0]


def in_token_order(places, parts, other, n_x):
    n_grp, tok = places.shape
    pieces, duo, blocks, run, width = other.shape
    count = 2 * pieces * blocks * run
    together = n_grp // duo

    def body(p_ref, *refs):
        o_ref, other_ref = refs[-1], refs[-2]
        for u in range(duo):
            rows = rows_by_core(refs[:-2], n_x, 0, (u,))
            rows += [other_ref[i, u] for i in range(pieces)]
            rows = jnp.concatenate([r.reshape(blocks * run, width) for r in rows], axis=0)
            for g in range(u * together, (u + 1) * together):
                onehot = jnp.concatenate(
                    [
                        onehot_of(p_ref[g : g + 1, t : t + LANES], count)
                        for t in range(0, tok, LANES)
                    ],
                    axis=0,
                )
                got = jnp.dot(onehot, rows, preferred_element_type=jnp.float32)
                o_ref[g] = got.astype(jnp.bfloat16)

    return near_call(body, [(n_grp, tok, width)], [places, *parts, other])[0]


def serve_and_project(stacked, hidden, w_proj, norm_gain):
    layers, rows, width = stacked.shape
    tok, depth = hidden.shape
    columns = w_proj.shape[1]
    steps = 5
    part = depth // steps

    def body(m_ref, h_hbm, w_ref, g_ref, s_ref, o_ref, *scratch):
        held, h_ref, weights, acc_ref, m_sem, s_sem, w_sem, h_sem = scratch
        loads, reads, writes = [], [], []
        states = pltpu.make_async_copy(h_hbm, h_ref, h_sem)
        states.start()
        for q in range(steps):
            rows_q = w_ref.at[q * part : (q + 1) * part]
            loads.append(pltpu.make_async_copy(rows_q, weights.at[q], w_sem.at[q]))
            loads[q].start()
        for l in range(layers):
            reads.append(pltpu.make_async_copy(m_ref.at[l], held.at[l], m_sem.at[l]))
            reads[l].start()
            block = s_ref.at[:, l * width : (l + 1) * width]
            writes.append(pltpu.make_async_copy(held.at[l], block, s_sem.at[l]))
        states.wait()
        for q in range(steps):
            loads[q].wait()
            term = jnp.dot(
                h_ref[:, q * part : (q + 1) * part],
                weights[q],
                preferred_element_type=jnp.float32,
            )
            if q:
                acc_ref[...] += term
            else:
                acc_ref[...] = term
        for l in range(layers):
            reads[l].wait()
            writes[l].start()
        for l in range(layers):
            proj = acc_ref[:, l * width : (l + 1) * width]
            mean_sq = jnp.mean(proj * proj, axis=-1, keepdims=True)
            o_ref[l] = proj / jnp.sqrt(mean_sq + 1e-06) * g_ref[...]
        for l in range(layers):
            writes[l].wait()

    hbm = pl.BlockSpec(memory_space=pltpu.HBM)
    vmem = pl.BlockSpec(memory_space=pltpu.VMEM)
    return pl.pallas_call(
        body,
        in_specs=[hbm, hbm, hbm, vmem],
        out_specs=[hbm, vmem],
        out_shape=[
            jax.ShapeDtypeStruct((rows, layers * width), stacked.dtype),
            jax.ShapeDtypeStruct((layers, tok, width), jnp.float32),
        ],
        scratch_shapes=[
            pltpu.VMEM((layers, rows, width), stacked.dtype),
            pltpu.VMEM((tok, depth), hidden.dtype),
            pltpu.VMEM((steps, part, columns), w_proj.dtype),
            pltpu.VMEM((tok, columns), jnp.float32),
            pltpu.SemaphoreType.DMA((layers,)),
            pltpu.SemaphoreType.DMA((layers,)),
            pltpu.SemaphoreType.DMA((steps,)),
            pltpu.SemaphoreType.DMA,
        ],
        compiler_params=pltpu.CompilerParams(vmem_limit_bytes=46 << 20),
        cost_estimate=pl.CostEstimate(
            flops=2 * tok * depth * columns,
            bytes_accessed=2 * depth * (tok + columns) + 4 * stacked.size,
            transcendentals=0,
        ),
    )(stacked, hidden, w_proj, norm_gain.reshape(1, width))


def add_embedding(crossed, pieces, normed):
    layers, tok, width = pieces.shape

    def body(s_ref, r_ref, *refs):
        n_refs, o_ref, acc_ref = refs[:-2], refs[-2], refs[-1]
        each = layers // len(n_refs)
        swap = s_ref[...] > 0
        for l in range(layers):
            emb = jnp.where(
                swap, r_ref[l ^ 1].astype(jnp.float32), r_ref[l].astype(jnp.float32)
            )
            acc_ref[:, l, :] = (n_refs[l // each][l % each] + math.sqrt(width) * emb) / math.sqrt(2.0)
        o_ref[...] = acc_ref[...].astype(jnp.bfloat16)

    vmem = pl.BlockSpec(memory_space=pltpu.VMEM)
    return pl.pallas_call(
        body,
        in_specs=[vmem] * (2 + len(normed)),
        out_specs=vmem,
        out_shape=jax.ShapeDtypeStruct((tok, layers, width), jnp.bfloat16),
        scratch_shapes=[pltpu.VMEM((tok, layers, width), jnp.float32)],
        compiler_params=pltpu.CompilerParams(vmem_limit_bytes=16 << 20),
        cost_estimate=pl.CostEstimate(
            flops=6 * tok * layers * width,
            bytes_accessed=8 * layers * width * tok,
            transcendentals=0,
        ),
    )(crossed.reshape(tok, 1), pieces, *normed)


def on_device(table, token_ids, hidden, w_proj, norm_gain):
    n_grp = lax.axis_size("grp")
    n_dev = lax.axis_size("dev")
    n_y, n_x = n_grp // 2, n_dev // 4
    peers = n_grp * n_dev
    d_index = lax.axis_index("dev")
    my_x, my_zh, my_c = d_index // 4, d_index // 2 % 2, d_index % 2
    _, shard_rows, width = table.shape
    layers = w_proj.shape[1] // width
    row_count = shard_rows // n_grp
    tok_count = token_ids.shape[0]
    slots = peers * CAP
    shard = table.reshape(shard_rows, width)
    hop = functools.partial(send, n_y=n_y, n_x=n_x)

    ids = lax.all_to_all(
        jnp.broadcast_to(token_ids[None, None], (n_grp, 1, tok_count)),
        "grp",
        split_axis=0,
        concat_axis=0,
        tiled=True,
    )
    gated, ids = lax.optimization_barrier((table.reshape(n_grp, row_count, width), ids))
    moved = lax.all_to_all(gated, "grp", split_axis=0, concat_axis=0, tiled=True)

    def crossed_of(holder):
        return (holder // 2 % 2) ^ my_zh

    ids = ids.reshape(n_grp, tok_count)
    block = ids // row_count
    positions = jnp.arange(tok_count, dtype=jnp.int32)
    same = (block[:, :, None] == block[:, None, :]) & (positions[None, :] < positions[:, None])
    rank = jnp.sum(same.astype(jnp.int32), axis=2)
    holder = block // n_grp
    k = (my_x - holder // 4 + n_x) % n_x
    in_shard = block % n_grp
    half_run = n_grp // 2 * CAP
    places = ((holder % 2) ^ my_c) * 2 + 1 - in_shard // (n_grp // 2)
    places = (places * 2 + crossed_of(holder)) * n_x + k
    spot = places * half_run + in_shard % (n_grp // 2) * CAP + rank
    odd = (jnp.arange(n_grp, dtype=jnp.int32) % 2)[:, None]
    places = (places * (n_grp // 2) + in_shard % (n_grp // 2)) * 2 * CAP + odd * CAP + rank
    hit = (spot[:, None, :] == jnp.arange(slots, dtype=jnp.int32)[None, :, None]).astype(
        jnp.int32
    )
    local = ids % row_count
    asked = jnp.sum(hit * (local + 1)[:, None, :], axis=2) - 1
    asked = asked.reshape(n_grp, 2, 2, 2, n_x, n_grp // 2, CAP).transpose(1, 3, 4, 2, 5, 0, 6)
    asked = asked.reshape(2, 2, n_x, n_grp, n_grp * CAP)
    asked = jnp.stack([asked[0], hop(asked[1], core=1)])
    asked = jnp.stack(
        [asked[:, :, 0]] + [hop(asked[:, :, q], dx=n_x - q) for q in range(1, n_x)]
    )
    asked = jnp.stack([asked[:, :, 0], hop(asked[:, :, 1], flip=1)], axis=1)
    wanted = asked.transpose(3, 0, 1, 2, 4).reshape(n_grp, n_x, 4 * n_grp * CAP)

    near, far = look_up(shard, wanted, n_x, n_grp, False)
    a_x = look_up(shard, wanted, n_x, n_grp, True)
    a_x = [a_x[0]] + [hop(a_x[q], dx=q) for q in range(1, n_x)]
    b_far = hop(far, flip=1)
    a_far = hop(flip_parts(a_x), flip=1)
    b_x = [hop(part, dx=q + 1) for q, part in enumerate(x_parts(near, b_far))]
    parts = [*a_x, a_far, near, b_far, *b_x]
    other = hop(core_parts(parts, n_x), core=1)
    sorted_rows = in_token_order(places, parts, other, n_x)
    moved, sorted_rows, hidden = lax.optimization_barrier((moved, sorted_rows, hidden))

    pieces = lax.all_to_all(sorted_rows, "grp", split_axis=0, concat_axis=0, tiled=True)
    served, normed = serve_and_project(moved, hidden, w_proj, norm_gain)
    served = served.reshape(1, 1, row_count, layers * width)
    crossed = crossed_of(token_ids // shard_rows)
    layer_inputs = add_embedding(crossed, pieces, [normed])
    return (served, layer_inputs)


def solution(mesh):
    in_specs = (P("grp", "dev", None), P(("grp", "dev")), P(("grp", "dev"), None), P(), P())
    out_specs = (P("dev", "grp", None, None), P(("grp", "dev"), None, None))
    return jax.shard_map(
        on_device, mesh=mesh, in_specs=in_specs, out_specs=out_specs, check_vma=False
    )
```

```python
import functools
import math

import jax
import jax.numpy as jnp
from jax import lax
from jax.experimental import pallas as pl
from jax.experimental.pallas import tpu as pltpu
from jax.sharding import PartitionSpec as P

CAP = 4
LANES = 128
BOTH = ("grp", "dev")


def flat_index(y, zl, x, zh, c, n_x):
    return (y * 2 + zl) * (n_x * 4) + x * 4 + zh * 2 + c


def send(value, n_y, n_x, dx=0, flip=0, core=0):
    moves = []
    for y in range(n_y):
        for x in range(n_x):
            for rest in range(8):
                zl, zh, c = rest // 4, rest // 2 % 2, rest % 2
                here = flat_index(y, zl, x, zh, c, n_x)
                there = flat_index(y, zl ^ flip, (x + dx) % n_x, zh ^ flip, c ^ core, n_x)
                moves.append((here, there))
    return lax.ppermute(value, BOTH, moves)


def column_of(line):
    lanes = line.shape[1]
    return jnp.transpose(jnp.broadcast_to(line, (lanes, lanes)))


def onehot_of(line, depth):
    col = column_of(line)
    lane = lax.broadcasted_iota(jnp.int32, col.shape, 1)
    return jnp.concatenate(
        [(col == lane + k * LANES).astype(jnp.bfloat16) for k in range(depth // LANES)], axis=1
    )


def look_up(shard, wanted, n_x, n_grp, x_first):
    blocks, lines, lanes = wanted.shape
    rows, width = shard.shape
    depth = rows // blocks
    half = blocks // 2
    duo = n_grp // 2
    outs = (n_x, 2) if x_first else (2, n_x)
    from_line, from_row = (0, half) if x_first else (half, 0)

    def body(w_ref, t_ref, *o_refs):
        for b in range(half):
            onehot = jnp.concatenate(
                [onehot_of(w_ref[from_line + b, r : r + 1, :], depth) for r in range(lines)],
                axis=0,
            )
            first = (from_row + b) * depth
            got = jnp.dot(
                onehot, t_ref[first : first + depth], preferred_element_type=jnp.float32
            )
            got = got.reshape(n_x, 2, 2, duo, 2 * CAP, width).astype(jnp.bfloat16)
            for k in range(n_x):
                for s in range(2):
                    if x_first:
                        o_refs[k][s, :, :, b] = got[k, s]
                    else:
                        o_refs[s][k, :, :, b] = got[k, s]

    shape = (outs[1], 2, duo, half, 2 * CAP, width)
    return near_call(body, [shape] * outs[0], [wanted, shard])


def near_call(body, outs, operands):
    vmem = pl.BlockSpec(memory_space=pltpu.VMEM)
    return pl.pallas_call(
        body,
        in_specs=[vmem] * len(operands),
        out_specs=[vmem] * len(outs),
        out_shape=[jax.ShapeDtypeStruct(shape, jnp.bfloat16) for shape in outs],
        compiler_params=pltpu.CompilerParams(vmem_limit_bytes=16 << 20),
        cost_estimate=pl.CostEstimate(flops=0, bytes_accessed=1 << 16, transcendentals=0),
    )(*operands)


def flip_parts(a_x):
    def body(*refs):
        for k, ref in enumerate(refs[:-1]):
            refs[-1][k] = ref[1]

    return near_call(body, [(len(a_x), *a_x[0].shape[1:])], a_x)[0]


def x_parts(near, b_far):
    n_x = near.shape[0]

    def body(n_ref, f_ref, *o_refs):
        for k, o_ref in enumerate(o_refs):
            o_ref[0] = n_ref[k + 1]
            o_ref[1] = f_ref[k + 1]

    return near_call(body, [(2, *near.shape[1:])] * (n_x - 1), [near, b_far])


def rows_by_core(refs, n_x, core, pick):
    a_refs, far_ref, near_ref, b_far_ref = refs[:n_x], refs[n_x], refs[n_x + 1], refs[n_x + 2]
    b_refs = refs[n_x + 3 : 2 * n_x + 2]
    rows = [r[(0, core) + pick] for r in a_refs]
    rows += [far_ref[(k, core) + pick] for k in range(n_x)]
    for s, ref in ((0, near_ref), (1, b_far_ref)):
        rows += [ref[(0, core) + pick]] + [r[(s, core) + pick] for r in b_refs]
    return rows


def core_parts(parts, n_x):
    def body(*refs):
        for i, rows in enumerate(rows_by_core(refs[:-1], n_x, 1, ())):
            refs[-1][i] = rows

    return near_call(body, [(4 * n_x, *parts[0].shape[2:])], parts)[0]


def in_token_order(places, parts, other, n_x):
    n_grp, tok = places.shape
    pieces, duo, blocks, run, width = other.shape
    count = 2 * pieces * blocks * run
    together = n_grp // duo

    def body(p_ref, *refs):
        o_ref, other_ref = refs[-1], refs[-2]
        for u in range(duo):
            rows = rows_by_core(refs[:-2], n_x, 0, (u,))
            rows += [other_ref[i, u] for i in range(pieces)]
            rows = jnp.concatenate([r.reshape(blocks * run, width) for r in rows], axis=0)
            for g in range(u * together, (u + 1) * together):
                onehot = jnp.concatenate(
                    [
                        onehot_of(p_ref[g : g + 1, t : t + LANES], count)
                        for t in range(0, tok, LANES)
                    ],
                    axis=0,
                )
                got = jnp.dot(onehot, rows, preferred_element_type=jnp.float32)
                o_ref[g] = got.astype(jnp.bfloat16)

    return near_call(body, [(n_grp, tok, width)], [places, *parts, other])[0]


def serve_and_project(stacked, hidden, w_proj, norm_gain):
    layers, rows, width = stacked.shape
    tok, depth = hidden.shape
    columns = w_proj.shape[1]
    steps = 5
    part = depth // steps

    def body(m_ref, h_hbm, w_ref, g_ref, s_ref, o_ref, *scratch):
        held, h_ref, weights, acc_ref, m_sem, s_sem, w_sem, h_sem = scratch
        loads, reads, writes = [], [], []
        states = pltpu.make_async_copy(h_hbm, h_ref, h_sem)
        states.start()
        for q in range(steps):
            rows_q = w_ref.at[q * part : (q + 1) * part]
            loads.append(pltpu.make_async_copy(rows_q, weights.at[q], w_sem.at[q]))
            loads[q].start()
        for l in range(layers):
            reads.append(pltpu.make_async_copy(m_ref.at[l], held.at[l], m_sem.at[l]))
            reads[l].start()
            block = s_ref.at[:, l * width : (l + 1) * width]
            writes.append(pltpu.make_async_copy(held.at[l], block, s_sem.at[l]))
        states.wait()
        for q in range(steps):
            loads[q].wait()
            term = jnp.dot(
                h_ref[:, q * part : (q + 1) * part],
                weights[q],
                preferred_element_type=jnp.float32,
            )
            if q:
                acc_ref[...] += term
            else:
                acc_ref[...] = term
        for l in range(layers):
            reads[l].wait()
            writes[l].start()
        for l in range(layers):
            proj = acc_ref[:, l * width : (l + 1) * width]
            mean_sq = jnp.mean(proj * proj, axis=-1, keepdims=True)
            o_ref[l] = proj / jnp.sqrt(mean_sq + 1e-06) * g_ref[...]
        for l in range(layers):
            writes[l].wait()

    hbm = pl.BlockSpec(memory_space=pltpu.HBM)
    vmem = pl.BlockSpec(memory_space=pltpu.VMEM)
    return pl.pallas_call(
        body,
        in_specs=[hbm, hbm, hbm, vmem],
        out_specs=[hbm, vmem],
        out_shape=[
            jax.ShapeDtypeStruct((rows, layers * width), stacked.dtype),
            jax.ShapeDtypeStruct((layers, tok, width), jnp.float32),
        ],
        scratch_shapes=[
            pltpu.VMEM((layers, rows, width), stacked.dtype),
            pltpu.VMEM((tok, depth), hidden.dtype),
            pltpu.VMEM((steps, part, columns), w_proj.dtype),
            pltpu.VMEM((tok, columns), jnp.float32),
            pltpu.SemaphoreType.DMA((layers,)),
            pltpu.SemaphoreType.DMA((layers,)),
            pltpu.SemaphoreType.DMA((steps,)),
            pltpu.SemaphoreType.DMA,
        ],
        compiler_params=pltpu.CompilerParams(vmem_limit_bytes=46 << 20),
        cost_estimate=pl.CostEstimate(
            flops=2 * tok * depth * columns,
            bytes_accessed=2 * depth * (tok + columns) + 4 * stacked.size,
            transcendentals=0,
        ),
    )(stacked, hidden, w_proj, norm_gain.reshape(1, width))


def add_embedding(crossed, pieces, normed):
    layers, tok, width = pieces.shape
    blocks = 4
    part = tok // blocks

    def body(s_ref, r_ref, n_ref, o_ref, acc_ref, out_ref, sem):
        copies = []
        for q in range(blocks):
            here = slice(q * part, (q + 1) * part)
            swap = s_ref[here] > 0
            for l in range(layers):
                emb = jnp.where(
                    swap,
                    r_ref[l ^ 1, here].astype(jnp.float32),
                    r_ref[l, here].astype(jnp.float32),
                )
                acc_ref[:, l, :] = (n_ref[l, here] + math.sqrt(width) * emb) / math.sqrt(2.0)
            out_ref[here] = acc_ref[...].astype(jnp.bfloat16)
            copies.append(pltpu.make_async_copy(out_ref.at[here], o_ref.at[here], sem.at[q]))
            copies[q].start()
        for copy in copies:
            copy.wait()

    vmem = pl.BlockSpec(memory_space=pltpu.VMEM)
    return pl.pallas_call(
        body,
        in_specs=[vmem] * 3,
        out_specs=pl.BlockSpec(memory_space=pltpu.HBM),
        out_shape=jax.ShapeDtypeStruct((tok, layers, width), jnp.bfloat16),
        scratch_shapes=[
            pltpu.VMEM((part, layers, width), jnp.float32),
            pltpu.VMEM((tok, layers, width), jnp.bfloat16),
            pltpu.SemaphoreType.DMA((blocks,)),
        ],
        compiler_params=pltpu.CompilerParams(vmem_limit_bytes=16 << 20),
        cost_estimate=pl.CostEstimate(
            flops=6 * tok * layers * width,
            bytes_accessed=8 * layers * width * tok,
            transcendentals=0,
        ),
    )(crossed.reshape(tok, 1), pieces, normed)


def on_device(table, token_ids, hidden, w_proj, norm_gain):
    n_grp = lax.axis_size("grp")
    n_dev = lax.axis_size("dev")
    n_y, n_x = n_grp // 2, n_dev // 4
    peers = n_grp * n_dev
    d_index = lax.axis_index("dev")
    my_x, my_zh, my_c = d_index // 4, d_index // 2 % 2, d_index % 2
    _, shard_rows, width = table.shape
    layers = w_proj.shape[1] // width
    row_count = shard_rows // n_grp
    tok_count = token_ids.shape[0]
    slots = peers * CAP
    shard = table.reshape(shard_rows, width)
    hop = functools.partial(send, n_y=n_y, n_x=n_x)

    columns = []
    for x in range(n_x):
        for c in range(2):
            columns.append(
                [
                    flat_index(g // 2, g % 2, x, zh, c, n_x)
                    for zh in range(2)
                    for g in range(n_grp)
                ]
            )
    ids = lax.all_to_all(
        jnp.broadcast_to(token_ids[None, None], (2 * n_grp, 1, tok_count)),
        BOTH,
        split_axis=0,
        concat_axis=0,
        axis_index_groups=columns,
        tiled=True,
    )
    gated, ids = lax.optimization_barrier((table.reshape(n_grp, row_count, width), ids))
    moved = lax.all_to_all(gated, "grp", split_axis=0, concat_axis=0, tiled=True)

    def crossed_of(holder):
        return (holder // 2 % 2) ^ my_zh

    ids = ids.reshape(2, n_grp, tok_count)
    ids = jnp.where(my_zh == 1, ids[::-1], ids)
    block = ids // row_count
    positions = jnp.arange(tok_count, dtype=jnp.int32)
    same = (block[..., :, None] == block[..., None, :]) & (
        positions[None, :] < positions[:, None]
    )
    rank = jnp.sum(same.astype(jnp.int32), axis=3)
    holder = block // n_grp
    k = (my_x - holder // 4 + n_x) % n_x
    in_shard = block % n_grp
    four = n_grp // 2
    part = ((holder % 2) ^ my_c) * 2 + 1 - in_shard // four
    spot = ((part * n_x + k) * four + in_shard % four) * CAP + rank
    spot = jnp.where(crossed_of(holder) == 0, spot, -1)
    odd = (jnp.arange(n_grp, dtype=jnp.int32) % 2)[:, None]
    places = ((part * 2 + crossed_of(holder)) * n_x + k) * four + in_shard % four
    places = places[0] * 2 * CAP + odd * CAP + rank[0]
    hit = (
        spot[:, :, None, :] == jnp.arange(slots // 2, dtype=jnp.int32)[None, None, :, None]
    ).astype(jnp.int32)
    local = ids % row_count
    asked = jnp.sum(hit * (local + 1)[:, :, None, :], axis=3) - 1
    asked = asked.reshape(2, n_grp, 2, 2, n_x, four, CAP).transpose(2, 0, 4, 3, 5, 1, 6)
    asked = asked.reshape(2, 2, n_x, n_grp, n_grp * CAP)
    asked = jnp.stack([asked[0], hop(asked[1], core=1)])
    asked = jnp.stack(
        [asked[:, :, 0]] + [hop(asked[:, :, q], dx=n_x - q) for q in range(1, n_x)]
    )
    wanted = asked.transpose(3, 0, 2, 1, 4).reshape(n_grp, n_x, 4 * n_grp * CAP)

    near, far = look_up(shard, wanted, n_x, n_grp, False)
    a_x = look_up(shard, wanted, n_x, n_grp, True)
    a_x = [a_x[0]] + [hop(a_x[q], dx=q) for q in range(1, n_x)]
    b_far = hop(far, flip=1)
    a_far = hop(flip_parts(a_x), flip=1)
    b_x = [hop(part, dx=q + 1) for q, part in enumerate(x_parts(near, b_far))]
    parts = [*a_x, a_far, near, b_far, *b_x]
    other = hop(core_parts(parts, n_x), core=1)
    sorted_rows = in_token_order(places, parts, other, n_x)
    moved, sorted_rows, hidden = lax.optimization_barrier((moved, sorted_rows, hidden))

    pieces = lax.all_to_all(sorted_rows, "grp", split_axis=0, concat_axis=0, tiled=True)
    served, normed = serve_and_project(moved, hidden, w_proj, norm_gain)
    served = served.reshape(1, 1, row_count, layers * width)
    crossed = crossed_of(token_ids // shard_rows)
    layer_inputs = add_embedding(crossed, pieces, normed)
    return (served, layer_inputs)


def solution(mesh):
    in_specs = (P("grp", "dev", None), P(("grp", "dev")), P(("grp", "dev"), None), P(), P())
    out_specs = (P("dev", "grp", None, None), P(("grp", "dev"), None, None))
    return jax.shard_map(
        on_device, mesh=mesh, in_specs=in_specs, out_specs=out_specs, check_vma=False
    )
```

```python
import functools
import math

import jax
import jax.numpy as jnp
from jax import lax
from jax.experimental import pallas as pl
from jax.experimental.pallas import tpu as pltpu
from jax.sharding import PartitionSpec as P

CAP = 4
LANES = 128
BOTH = ("grp", "dev")


def flat_index(y, zl, x, zh, c, n_x):
    return (y * 2 + zl) * (n_x * 4) + x * 4 + zh * 2 + c


def send(value, n_y, n_x, dx=0, flip=0, core=0):
    moves = []
    for y in range(n_y):
        for x in range(n_x):
            for rest in range(8):
                zl, zh, c = rest // 4, rest // 2 % 2, rest % 2
                here = flat_index(y, zl, x, zh, c, n_x)
                there = flat_index(y, zl ^ flip, (x + dx) % n_x, zh ^ flip, c ^ core, n_x)
                moves.append((here, there))
    return lax.ppermute(value, BOTH, moves)


def column_of(line):
    lanes = line.shape[1]
    return jnp.transpose(jnp.broadcast_to(line, (lanes, lanes)))


def onehot_of(line, depth):
    col = column_of(line)
    lane = lax.broadcasted_iota(jnp.int32, col.shape, 1)
    return jnp.concatenate(
        [(col == lane + k * LANES).astype(jnp.bfloat16) for k in range(depth // LANES)], axis=1
    )


def look_up(shard, wanted, n_x, n_grp, x_first):
    blocks, lines, lanes = wanted.shape
    rows, width = shard.shape
    depth = rows // blocks
    half = blocks // 2
    duo = n_grp // 2
    outs = (n_x, 2) if x_first else (2, n_x)
    from_line, from_row = (0, half) if x_first else (half, 0)

    def body(w_ref, t_ref, *o_refs):
        for b in range(half):
            onehot = jnp.concatenate(
                [onehot_of(w_ref[from_line + b, r : r + 1, :], depth) for r in range(lines)],
                axis=0,
            )
            first = (from_row + b) * depth
            got = jnp.dot(
                onehot, t_ref[first : first + depth], preferred_element_type=jnp.float32
            )
            got = got.reshape(n_x, 2, 2, duo, 2 * CAP, width).astype(jnp.bfloat16)
            for k in range(n_x):
                for s in range(2):
                    if x_first:
                        o_refs[k][s, :, :, b] = got[k, s]
                    else:
                        o_refs[s][k, :, :, b] = got[k, s]

    shape = (outs[1], 2, duo, half, 2 * CAP, width)
    return near_call(body, [shape] * outs[0], [wanted, shard])


def near_call(body, outs, operands):
    vmem = pl.BlockSpec(memory_space=pltpu.VMEM)
    return pl.pallas_call(
        body,
        in_specs=[vmem] * len(operands),
        out_specs=[vmem] * len(outs),
        out_shape=[jax.ShapeDtypeStruct(shape, jnp.bfloat16) for shape in outs],
        compiler_params=pltpu.CompilerParams(vmem_limit_bytes=16 << 20),
        cost_estimate=pl.CostEstimate(flops=0, bytes_accessed=1 << 16, transcendentals=0),
    )(*operands)


def flip_parts(a_x):
    def body(*refs):
        for k, ref in enumerate(refs[:-1]):
            refs[-1][k] = ref[1]

    return near_call(body, [(len(a_x), *a_x[0].shape[1:])], a_x)[0]


def x_parts(near, b_far):
    n_x = near.shape[0]

    def body(n_ref, f_ref, *o_refs):
        for k, o_ref in enumerate(o_refs):
            o_ref[0] = n_ref[k + 1]
            o_ref[1] = f_ref[k + 1]

    return near_call(body, [(2, *near.shape[1:])] * (n_x - 1), [near, b_far])


def rows_by_core(refs, n_x, core, pick):
    a_refs, far_ref, near_ref, b_far_ref = refs[:n_x], refs[n_x], refs[n_x + 1], refs[n_x + 2]
    b_refs = refs[n_x + 3 : 2 * n_x + 2]
    rows = [r[(0, core) + pick] for r in a_refs]
    rows += [far_ref[(k, core) + pick] for k in range(n_x)]
    for s, ref in ((0, near_ref), (1, b_far_ref)):
        rows += [ref[(0, core) + pick]] + [r[(s, core) + pick] for r in b_refs]
    return rows


def core_parts(parts, n_x):
    def body(*refs):
        for i, rows in enumerate(rows_by_core(refs[:-1], n_x, 1, ())):
            refs[-1][i] = rows

    return near_call(body, [(4 * n_x, *parts[0].shape[2:])], parts)[0]


def in_token_order(places, parts, other, n_x):
    n_grp, tok = places.shape
    pieces, duo, blocks, run, width = other.shape
    count = 2 * pieces * blocks * run
    together = n_grp // duo

    def body(p_ref, *refs):
        o_ref, other_ref = refs[-1], refs[-2]
        for u in range(duo):
            rows = rows_by_core(refs[:-2], n_x, 0, (u,))
            rows += [other_ref[i, u] for i in range(pieces)]
            rows = jnp.concatenate([r.reshape(blocks * run, width) for r in rows], axis=0)
            for g in range(u * together, (u + 1) * together):
                onehot = jnp.concatenate(
                    [
                        onehot_of(p_ref[g : g + 1, t : t + LANES], count)
                        for t in range(0, tok, LANES)
                    ],
                    axis=0,
                )
                got = jnp.dot(onehot, rows, preferred_element_type=jnp.float32)
                o_ref[g] = got.astype(jnp.bfloat16)

    return near_call(body, [(n_grp, tok, width)], [places, *parts, other])[0]


def serve_and_project(stacked, hidden, w_proj, norm_gain):
    layers, rows, width = stacked.shape
    tok, depth = hidden.shape
    columns = w_proj.shape[1]
    steps = 5
    part = depth // steps

    def body(m_ref, h_hbm, w_ref, g_ref, s_ref, o_ref, *scratch):
        held, h_ref, weights, acc_ref, m_sem, s_sem, w_sem, h_sem = scratch
        loads, reads, writes = [], [], []
        states = pltpu.make_async_copy(h_hbm, h_ref, h_sem)
        states.start()
        for q in range(steps):
            rows_q = w_ref.at[q * part : (q + 1) * part]
            loads.append(pltpu.make_async_copy(rows_q, weights.at[q], w_sem.at[q]))
            loads[q].start()
        for l in range(layers):
            reads.append(pltpu.make_async_copy(m_ref.at[l], held.at[l], m_sem.at[l]))
            reads[l].start()
            block = s_ref.at[:, l * width : (l + 1) * width]
            writes.append(pltpu.make_async_copy(held.at[l], block, s_sem.at[l]))
        states.wait()
        for q in range(steps):
            loads[q].wait()
            term = jnp.dot(
                h_ref[:, q * part : (q + 1) * part],
                weights[q],
                preferred_element_type=jnp.float32,
            )
            if q:
                acc_ref[...] += term
            else:
                acc_ref[...] = term
        for l in range(layers):
            reads[l].wait()
            writes[l].start()
        for l in range(layers):
            proj = acc_ref[:, l * width : (l + 1) * width]
            mean_sq = jnp.mean(proj * proj, axis=-1, keepdims=True)
            normed = proj / jnp.sqrt(mean_sq + 1e-06) * g_ref[...]
            o_ref[l] = normed / math.sqrt(2.0)
        for l in range(layers):
            writes[l].wait()

    hbm = pl.BlockSpec(memory_space=pltpu.HBM)
    vmem = pl.BlockSpec(memory_space=pltpu.VMEM)
    return pl.pallas_call(
        body,
        in_specs=[hbm, hbm, hbm, vmem],
        out_specs=[hbm, vmem],
        out_shape=[
            jax.ShapeDtypeStruct((rows, layers * width), stacked.dtype),
            jax.ShapeDtypeStruct((layers, tok, width), jnp.float32),
        ],
        scratch_shapes=[
            pltpu.VMEM((layers, rows, width), stacked.dtype),
            pltpu.VMEM((tok, depth), hidden.dtype),
            pltpu.VMEM((steps, part, columns), w_proj.dtype),
            pltpu.VMEM((tok, columns), jnp.float32),
            pltpu.SemaphoreType.DMA((layers,)),
            pltpu.SemaphoreType.DMA((layers,)),
            pltpu.SemaphoreType.DMA((steps,)),
            pltpu.SemaphoreType.DMA,
        ],
        compiler_params=pltpu.CompilerParams(vmem_limit_bytes=46 << 20),
        cost_estimate=pl.CostEstimate(
            flops=2 * tok * depth * columns,
            bytes_accessed=2 * depth * (tok + columns) + 4 * stacked.size,
            transcendentals=0,
        ),
    )(stacked, hidden, w_proj, norm_gain.reshape(1, width))


def add_embedding(crossed, pieces, normed):
    layers, tok, width = pieces.shape
    blocks = 4
    part = tok // blocks

    def body(s_ref, r_ref, n_ref, o_ref, acc_ref, out_ref, sem):
        copies = []
        for q in range(blocks):
            here = slice(q * part, (q + 1) * part)
            swap = s_ref[here] > 0
            for l in range(layers):
                emb = jnp.where(
                    swap,
                    r_ref[l ^ 1, here].astype(jnp.float32),
                    r_ref[l, here].astype(jnp.float32),
                )
                acc_ref[:, l, :] = n_ref[l, here] + math.sqrt(width / 2.0) * emb
            out_ref[here] = acc_ref[...].astype(jnp.bfloat16)
            copies.append(pltpu.make_async_copy(out_ref.at[here], o_ref.at[here], sem.at[q]))
            copies[q].start()
        for copy in copies:
            copy.wait()

    vmem = pl.BlockSpec(memory_space=pltpu.VMEM)
    return pl.pallas_call(
        body,
        in_specs=[vmem] * 3,
        out_specs=pl.BlockSpec(memory_space=pltpu.HBM),
        out_shape=jax.ShapeDtypeStruct((tok, layers, width), jnp.bfloat16),
        scratch_shapes=[
            pltpu.VMEM((part, layers, width), jnp.float32),
            pltpu.VMEM((tok, layers, width), jnp.bfloat16),
            pltpu.SemaphoreType.DMA((blocks,)),
        ],
        compiler_params=pltpu.CompilerParams(vmem_limit_bytes=16 << 20),
        cost_estimate=pl.CostEstimate(
            flops=6 * tok * layers * width,
            bytes_accessed=8 * layers * width * tok,
            transcendentals=0,
        ),
    )(crossed.reshape(tok, 1), pieces, normed)


def on_device(table, token_ids, hidden, w_proj, norm_gain):
    n_grp = lax.axis_size("grp")
    n_dev = lax.axis_size("dev")
    n_y, n_x = n_grp // 2, n_dev // 4
    peers = n_grp * n_dev
    d_index = lax.axis_index("dev")
    my_x, my_zh, my_c = d_index // 4, d_index // 2 % 2, d_index % 2
    _, shard_rows, width = table.shape
    layers = w_proj.shape[1] // width
    row_count = shard_rows // n_grp
    tok_count = token_ids.shape[0]
    slots = peers * CAP
    shard = table.reshape(shard_rows, width)
    hop = functools.partial(send, n_y=n_y, n_x=n_x)

    columns = []
    for x in range(n_x):
        for c in range(2):
            columns.append(
                [
                    flat_index(g // 2, g % 2, x, zh, c, n_x)
                    for zh in range(2)
                    for g in range(n_grp)
                ]
            )
    ids = lax.all_to_all(
        jnp.broadcast_to(token_ids[None, None], (2 * n_grp, 1, tok_count)),
        BOTH,
        split_axis=0,
        concat_axis=0,
        axis_index_groups=columns,
        tiled=True,
    )
    gated, ids = lax.optimization_barrier((table.reshape(n_grp, row_count, width), ids))
    moved = lax.all_to_all(gated, "grp", split_axis=0, concat_axis=0, tiled=True)

    def crossed_of(holder):
        return (holder // 2 % 2) ^ my_zh

    ids = ids.reshape(2, n_grp, tok_count)
    ids = jnp.where(my_zh == 1, ids[::-1], ids)
    block = ids // row_count
    positions = jnp.arange(tok_count, dtype=jnp.int32)
    same = (block[..., :, None] == block[..., None, :]) & (
        positions[None, :] < positions[:, None]
    )
    rank = jnp.sum(same.astype(jnp.int32), axis=3)
    holder = block // n_grp
    k = (my_x - holder // 4 + n_x) % n_x
    in_shard = block % n_grp
    four = n_grp // 2
    part = ((holder % 2) ^ my_c) * 2 + 1 - in_shard // four
    spot = ((part * n_x + k) * four + in_shard % four) * CAP + rank
    spot = jnp.where(crossed_of(holder) == 0, spot, -1)
    odd = (jnp.arange(n_grp, dtype=jnp.int32) % 2)[:, None]
    places = ((part * 2 + crossed_of(holder)) * n_x + k) * four + in_shard % four
    places = places[0] * 2 * CAP + odd * CAP + rank[0]
    hit = (
        spot[:, :, None, :] == jnp.arange(slots // 2, dtype=jnp.int32)[None, None, :, None]
    ).astype(jnp.int32)
    local = ids % row_count
    asked = jnp.sum(hit * (local + 1)[:, :, None, :], axis=3) - 1
    asked = asked.reshape(2, n_grp, 2, 2, n_x, four, CAP).transpose(2, 0, 4, 3, 5, 1, 6)
    asked = asked.reshape(2, 2, n_x, n_grp, n_grp * CAP)
    asked = jnp.stack([asked[0], hop(asked[1], core=1)])
    asked = jnp.stack(
        [asked[:, :, 0]] + [hop(asked[:, :, q], dx=n_x - q) for q in range(1, n_x)]
    )
    wanted = asked.transpose(3, 0, 2, 1, 4).reshape(n_grp, n_x, 4 * n_grp * CAP)

    near, far = look_up(shard, wanted, n_x, n_grp, False)
    a_x = look_up(shard, wanted, n_x, n_grp, True)
    a_x = [a_x[0]] + [hop(a_x[q], dx=q) for q in range(1, n_x)]
    b_far = hop(far, flip=1)
    a_far = hop(flip_parts(a_x), flip=1)
    b_x = [hop(part, dx=q + 1) for q, part in enumerate(x_parts(near, b_far))]
    parts = [*a_x, a_far, near, b_far, *b_x]
    other = hop(core_parts(parts, n_x), core=1)
    sorted_rows = in_token_order(places, parts, other, n_x)
    moved, sorted_rows, hidden = lax.optimization_barrier((moved, sorted_rows, hidden))

    pieces = lax.all_to_all(sorted_rows, "grp", split_axis=0, concat_axis=0, tiled=True)
    served, normed = serve_and_project(moved, hidden, w_proj, norm_gain)
    served = served.reshape(1, 1, row_count, layers * width)
    crossed = crossed_of(token_ids // shard_rows)
    layer_inputs = add_embedding(crossed, pieces, normed)
    return (served, layer_inputs)


def solution(mesh):
    in_specs = (P("grp", "dev", None), P(("grp", "dev")), P(("grp", "dev"), None), P(), P())
    out_specs = (P("dev", "grp", None, None), P(("grp", "dev"), None, None))
    return jax.shard_map(
        on_device, mesh=mesh, in_specs=in_specs, out_specs=out_specs, check_vma=False
    )
```

```python
import functools
import math

import jax
import jax.numpy as jnp
from jax import lax
from jax.experimental import pallas as pl
from jax.experimental.pallas import tpu as pltpu
from jax.sharding import PartitionSpec as P

CAP = 4
LANES = 128
BOTH = ("grp", "dev")


def flat_index(y, zl, x, zh, c, n_x):
    return (y * 2 + zl) * (n_x * 4) + x * 4 + zh * 2 + c


def send(value, n_y, n_x, dx=0, flip=0, core=0):
    moves = []
    for y in range(n_y):
        for x in range(n_x):
            for rest in range(8):
                zl, zh, c = rest // 4, rest // 2 % 2, rest % 2
                here = flat_index(y, zl, x, zh, c, n_x)
                there = flat_index(y, zl ^ flip, (x + dx) % n_x, zh ^ flip, c ^ core, n_x)
                moves.append((here, there))
    return lax.ppermute(value, BOTH, moves)


def column_of(line):
    lanes = line.shape[1]
    return jnp.transpose(jnp.broadcast_to(line, (lanes, lanes)))


def onehot_of(line, depth):
    col = column_of(line)
    lane = lax.broadcasted_iota(jnp.int32, col.shape, 1)
    return jnp.concatenate(
        [(col == lane + k * LANES).astype(jnp.bfloat16) for k in range(depth // LANES)], axis=1
    )


def look_up(shard, wanted, n_x, n_grp, x_first):
    blocks, lines, lanes = wanted.shape
    rows, width = shard.shape
    depth = rows // blocks
    half = blocks // 2
    duo = n_grp // 2
    outs = (n_x, 2) if x_first else (2, n_x)
    from_line, from_row = (0, half) if x_first else (half, 0)

    def body(w_ref, t_ref, *o_refs):
        for b in range(half):
            onehot = jnp.concatenate(
                [onehot_of(w_ref[from_line + b, r : r + 1, :], depth) for r in range(lines)],
                axis=0,
            )
            first = (from_row + b) * depth
            got = jnp.dot(
                onehot, t_ref[first : first + depth], preferred_element_type=jnp.float32
            )
            got = got.reshape(n_x, 2, 2, duo, 2 * CAP, width).astype(jnp.bfloat16)
            for k in range(n_x):
                for s in range(2):
                    if x_first:
                        o_refs[k][s, :, :, b] = got[k, s]
                    else:
                        o_refs[s][k, :, :, b] = got[k, s]

    shape = (outs[1], 2, duo, half, 2 * CAP, width)
    return near_call(body, [shape] * outs[0], [wanted, shard])


def near_call(body, outs, operands):
    vmem = pl.BlockSpec(memory_space=pltpu.VMEM)
    return pl.pallas_call(
        body,
        in_specs=[vmem] * len(operands),
        out_specs=[vmem] * len(outs),
        out_shape=[jax.ShapeDtypeStruct(shape, jnp.bfloat16) for shape in outs],
        compiler_params=pltpu.CompilerParams(vmem_limit_bytes=16 << 20),
        cost_estimate=pl.CostEstimate(flops=0, bytes_accessed=1 << 16, transcendentals=0),
    )(*operands)


def flip_parts(a_x):
    def body(*refs):
        for k, ref in enumerate(refs[:-1]):
            refs[-1][k] = ref[1]

    return near_call(body, [(len(a_x), *a_x[0].shape[1:])], a_x)[0]


def x_parts(near, b_far):
    n_x = near.shape[0]

    def body(n_ref, f_ref, *o_refs):
        for k, o_ref in enumerate(o_refs):
            o_ref[0] = n_ref[k + 1]
            o_ref[1] = f_ref[k + 1]

    return near_call(body, [(2, *near.shape[1:])] * (n_x - 1), [near, b_far])


def rows_by_core(refs, n_x, core, pick):
    a_refs, far_ref, near_ref, b_far_ref = refs[:n_x], refs[n_x], refs[n_x + 1], refs[n_x + 2]
    b_refs = refs[n_x + 3 : 2 * n_x + 2]
    rows = [r[(0, core) + pick] for r in a_refs]
    rows += [far_ref[(k, core) + pick] for k in range(n_x)]
    for s, ref in ((0, near_ref), (1, b_far_ref)):
        rows += [ref[(0, core) + pick]] + [r[(s, core) + pick] for r in b_refs]
    return rows


def core_parts(parts, n_x):
    def body(*refs):
        for i, rows in enumerate(rows_by_core(refs[:-1], n_x, 1, ())):
            refs[-1][i] = rows

    return near_call(body, [(4 * n_x, *parts[0].shape[2:])], parts)[0]


def in_token_order(places, parts, other, n_x):
    n_grp, tok = places.shape
    pieces, duo, blocks, run, width = other.shape
    count = 2 * pieces * blocks * run
    together = n_grp // duo

    def body(p_ref, *refs):
        o_ref, other_ref = refs[-1], refs[-2]
        for u in range(duo):
            rows = rows_by_core(refs[:-2], n_x, 0, (u,))
            rows += [other_ref[i, u] for i in range(pieces)]
            rows = jnp.concatenate([r.reshape(blocks * run, width) for r in rows], axis=0)
            for g in range(u * together, (u + 1) * together):
                onehot = jnp.concatenate(
                    [
                        onehot_of(p_ref[g : g + 1, t : t + LANES], count)
                        for t in range(0, tok, LANES)
                    ],
                    axis=0,
                )
                got = jnp.dot(onehot, rows, preferred_element_type=jnp.float32)
                o_ref[g] = got.astype(jnp.bfloat16)

    return near_call(body, [(n_grp, tok, width)], [places, *parts, other])[0]


def serve(stacked):
    layers, rows, width = stacked.shape

    def body(m_ref, s_ref, held, m_sem, s_sem):
        reads, writes = [], []
        for l in range(layers):
            reads.append(pltpu.make_async_copy(m_ref.at[l], held.at[l], m_sem.at[l]))
            reads[l].start()
            block = s_ref.at[:, l * width : (l + 1) * width]
            writes.append(pltpu.make_async_copy(held.at[l], block, s_sem.at[l]))
        for l in range(layers):
            reads[l].wait()
            writes[l].start()
        for write in writes:
            write.wait()

    hbm = pl.BlockSpec(memory_space=pltpu.HBM)
    return pl.pallas_call(
        body,
        in_specs=[hbm],
        out_specs=hbm,
        out_shape=jax.ShapeDtypeStruct((rows, layers * width), stacked.dtype),
        scratch_shapes=[
            pltpu.VMEM((layers, rows, width), stacked.dtype),
            pltpu.SemaphoreType.DMA((layers,)),
            pltpu.SemaphoreType.DMA((layers,)),
        ],
        compiler_params=pltpu.CompilerParams(vmem_limit_bytes=16 << 20),
        cost_estimate=pl.CostEstimate(
            flops=0, bytes_accessed=4 * stacked.size, transcendentals=0
        ),
    )(stacked)


def normed_projection(hidden, w_proj, norm_gain, layers):
    tok, depth = hidden.shape
    columns = w_proj.shape[1]
    width = columns // layers
    steps = 5
    part = depth // steps

    def body(h_hbm, w_ref, g_ref, o_ref, h_ref, weights, acc_ref, w_sem, h_sem):
        loads = []
        states = pltpu.make_async_copy(h_hbm, h_ref, h_sem)
        states.start()
        for q in range(steps):
            rows_q = w_ref.at[q * part : (q + 1) * part]
            loads.append(pltpu.make_async_copy(rows_q, weights.at[q], w_sem.at[q]))
            loads[q].start()
        states.wait()
        for q in range(steps):
            loads[q].wait()
            term = jnp.dot(
                h_ref[:, q * part : (q + 1) * part],
                weights[q],
                preferred_element_type=jnp.float32,
            )
            if q:
                acc_ref[...] += term
            else:
                acc_ref[...] = term
        for l in range(layers):
            proj = acc_ref[:, l * width : (l + 1) * width]
            mean_sq = jnp.mean(proj * proj, axis=-1, keepdims=True)
            normed = proj / jnp.sqrt(mean_sq + 1e-06) * g_ref[...]
            o_ref[l] = normed / math.sqrt(2.0)

    hbm = pl.BlockSpec(memory_space=pltpu.HBM)
    vmem = pl.BlockSpec(memory_space=pltpu.VMEM)
    return pl.pallas_call(
        body,
        in_specs=[hbm, hbm, vmem],
        out_specs=vmem,
        out_shape=jax.ShapeDtypeStruct((layers, tok, width), jnp.float32),
        scratch_shapes=[
            pltpu.VMEM((tok, depth), hidden.dtype),
            pltpu.VMEM((steps, part, columns), w_proj.dtype),
            pltpu.VMEM((tok, columns), jnp.float32),
            pltpu.SemaphoreType.DMA((steps,)),
            pltpu.SemaphoreType.DMA,
        ],
        compiler_params=pltpu.CompilerParams(vmem_limit_bytes=56 << 20),
        cost_estimate=pl.CostEstimate(
            flops=2 * tok * depth * columns,
            bytes_accessed=2 * depth * (tok + columns) + 4 * tok * columns,
            transcendentals=0,
        ),
    )(hidden, w_proj, norm_gain.reshape(1, width))


def add_embedding(crossed, pieces, normed):
    layers, tok, width = pieces.shape
    blocks = 4
    part = tok // blocks

    def body(s_ref, r_ref, n_ref, o_ref, acc_ref, out_ref, sem):
        copies = []
        for q in range(blocks):
            here = slice(q * part, (q + 1) * part)
            swap = s_ref[here] > 0
            for l in range(layers):
                emb = jnp.where(
                    swap,
                    r_ref[l ^ 1, here].astype(jnp.float32),
                    r_ref[l, here].astype(jnp.float32),
                )
                acc_ref[:, l, :] = n_ref[l, here] + math.sqrt(width / 2.0) * emb
            out_ref[here] = acc_ref[...].astype(jnp.bfloat16)
            copies.append(pltpu.make_async_copy(out_ref.at[here], o_ref.at[here], sem.at[q]))
            copies[q].start()
        for copy in copies:
            copy.wait()

    vmem = pl.BlockSpec(memory_space=pltpu.VMEM)
    return pl.pallas_call(
        body,
        in_specs=[vmem] * 3,
        out_specs=pl.BlockSpec(memory_space=pltpu.HBM),
        out_shape=jax.ShapeDtypeStruct((tok, layers, width), jnp.bfloat16),
        scratch_shapes=[
            pltpu.VMEM((part, layers, width), jnp.float32),
            pltpu.VMEM((tok, layers, width), jnp.bfloat16),
            pltpu.SemaphoreType.DMA((blocks,)),
        ],
        compiler_params=pltpu.CompilerParams(vmem_limit_bytes=16 << 20),
        cost_estimate=pl.CostEstimate(
            flops=6 * tok * layers * width,
            bytes_accessed=8 * layers * width * tok,
            transcendentals=0,
        ),
    )(crossed.reshape(tok, 1), pieces, normed)


def on_device(table, token_ids, hidden, w_proj, norm_gain):
    n_grp = lax.axis_size("grp")
    n_dev = lax.axis_size("dev")
    n_y, n_x = n_grp // 2, n_dev // 4
    peers = n_grp * n_dev
    d_index = lax.axis_index("dev")
    my_x, my_zh, my_c = d_index // 4, d_index // 2 % 2, d_index % 2
    _, shard_rows, width = table.shape
    layers = w_proj.shape[1] // width
    row_count = shard_rows // n_grp
    tok_count = token_ids.shape[0]
    slots = peers * CAP
    shard = table.reshape(shard_rows, width)
    hop = functools.partial(send, n_y=n_y, n_x=n_x)

    columns = []
    for x in range(n_x):
        for c in range(2):
            columns.append(
                [
                    flat_index(g // 2, g % 2, x, zh, c, n_x)
                    for zh in range(2)
                    for g in range(n_grp)
                ]
            )
    ids = lax.all_to_all(
        jnp.broadcast_to(token_ids[None, None], (2 * n_grp, 1, tok_count)),
        BOTH,
        split_axis=0,
        concat_axis=0,
        axis_index_groups=columns,
        tiled=True,
    )
    normed = normed_projection(hidden, w_proj, norm_gain, layers)
    gated, ids, normed = lax.optimization_barrier(
        (table.reshape(n_grp, row_count, width), ids, normed)
    )
    moved = lax.all_to_all(gated, "grp", split_axis=0, concat_axis=0, tiled=True)

    def crossed_of(holder):
        return (holder // 2 % 2) ^ my_zh

    ids = ids.reshape(2, n_grp, tok_count)
    ids = jnp.where(my_zh == 1, ids[::-1], ids)
    block = ids // row_count
    positions = jnp.arange(tok_count, dtype=jnp.int32)
    same = (block[..., :, None] == block[..., None, :]) & (
        positions[None, :] < positions[:, None]
    )
    rank = jnp.sum(same.astype(jnp.int32), axis=3)
    holder = block // n_grp
    k = (my_x - holder // 4 + n_x) % n_x
    in_shard = block % n_grp
    four = n_grp // 2
    part = ((holder % 2) ^ my_c) * 2 + 1 - in_shard // four
    spot = ((part * n_x + k) * four + in_shard % four) * CAP + rank
    spot = jnp.where(crossed_of(holder) == 0, spot, -1)
    odd = (jnp.arange(n_grp, dtype=jnp.int32) % 2)[:, None]
    places = ((part * 2 + crossed_of(holder)) * n_x + k) * four + in_shard % four
    places = places[0] * 2 * CAP + odd * CAP + rank[0]
    hit = (
        spot[:, :, None, :] == jnp.arange(slots // 2, dtype=jnp.int32)[None, None, :, None]
    ).astype(jnp.int32)
    local = ids % row_count
    asked = jnp.sum(hit * (local + 1)[:, :, None, :], axis=3) - 1
    asked = asked.reshape(2, n_grp, 2, 2, n_x, four, CAP).transpose(2, 0, 4, 3, 5, 1, 6)
    asked = asked.reshape(2, 2, n_x, n_grp, n_grp * CAP)
    asked = jnp.stack([asked[0], hop(asked[1], core=1)])
    asked = jnp.stack(
        [asked[:, :, 0]] + [hop(asked[:, :, q], dx=n_x - q) for q in range(1, n_x)]
    )
    wanted = asked.transpose(3, 0, 2, 1, 4).reshape(n_grp, n_x, 4 * n_grp * CAP)

    near, far = look_up(shard, wanted, n_x, n_grp, False)
    a_x = look_up(shard, wanted, n_x, n_grp, True)
    a_x = [a_x[0]] + [hop(a_x[q], dx=q) for q in range(1, n_x)]
    b_far = hop(far, flip=1)
    a_far = hop(flip_parts(a_x), flip=1)
    b_x = [hop(part, dx=q + 1) for q, part in enumerate(x_parts(near, b_far))]
    parts = [*a_x, a_far, near, b_far, *b_x]
    other = hop(core_parts(parts, n_x), core=1)
    sorted_rows = in_token_order(places, parts, other, n_x)
    moved, sorted_rows = lax.optimization_barrier((moved, sorted_rows))

    pieces = lax.all_to_all(sorted_rows, "grp", split_axis=0, concat_axis=0, tiled=True)
    served = serve(moved).reshape(1, 1, row_count, layers * width)
    crossed = crossed_of(token_ids // shard_rows)
    layer_inputs = add_embedding(crossed, pieces, normed)
    return (served, layer_inputs)


def solution(mesh):
    in_specs = (P("grp", "dev", None), P(("grp", "dev")), P(("grp", "dev"), None), P(), P())
    out_specs = (P("dev", "grp", None, None), P(("grp", "dev"), None, None))
    return jax.shard_map(
        on_device, mesh=mesh, in_specs=in_specs, out_specs=out_specs, check_vma=False
    )
```
